128 devices in a mesh: src: 16 (over y_lo, z, core), rcv: 8 (over x, y_hi).
Axes of the slice: x: 4, y: 4 (y_hi: 2, y_lo: 2; y = y_hi * 2 + y_lo), z: 4, core: 2. Of those that a mesh axis runs over, the one named last changes fastest.
Arguments:
- traces: float32 [1024, 1024, 512], P(('src', 'rcv')), may hold values from -6 to 6
- sketch: float32 [1024, 64], replicated, may hold values from -0.1875 to 0.1875
Outputs:
- range_basis: float32 [32, 2, 1024, 64], P('rcv', None, 'src')
- r_factor: float32 [32, 64, 64], P('rcv')
The draws below stay inside these ranges and needn't reach their ends.
All inputs are finite; a program needn't handle non-finite values.
Results may differ from the reference program's by a relative error of at most 0.0003.
Values sent between devices are 32-bit elements; how exact they have to be, the bound alone decides.
No kernel may reach another device: no remote copies, remote signals or barrier semaphores. Data moves between devices by JAX's collectives and lax.ppermute only.
A program may use at most 128 MiB of HBM per device.

```python
import math
import jax
import jax.numpy as jnp
from jax import lax

NT = 512
FREQS = 32
RANK = 64
N = 1024


def shard_levels(rng, shape, pieces, low, high):
    level = 1.0
    for dim, blocks in pieces:
        steps = jax.random.uniform(jax.random.fold_in(jax.random.fold_in(rng, 6), dim), (blocks,), jnp.float32, low / len(pieces), high / len(pieces))
        level = level * jnp.repeat(jnp.exp(steps), shape[dim] // blocks).reshape((-1,) + (1,) * (len(shape) - 1 - dim))
    return level


def scatter_about(rng, shape, scale, bound, cuts=(), kind=jnp.bfloat16):
    entries = jax.random.normal(rng, shape, jnp.float32) * scale
    if len(cuts) > 0:
        entries = shard_levels(rng, shape, cuts, -0.22, 0.18) * entries
    return jnp.clip(entries, min=-bound, max=bound).astype(kind)


def setup_inputs(seed: int = 0) -> dict:
    key_of = jax.random.split(jax.random.key(seed), 3)
    traces = scatter_about(key_of[0], (N, N, NT), 1.0, 6.0, ((0, 128),), jnp.float32)
    sketch = scatter_about(key_of[1], (N, RANK), N ** -0.5, 0.1875, (), jnp.float32)
    return dict(traces=traces, sketch=sketch)


def dft_rows(samples):
    time_index = jnp.arange(samples, dtype=jnp.int32)
    orders = jnp.arange(1, FREQS + 1, dtype=jnp.int32)
    phases = orders[:, None] * time_index[None, :] % samples
    angles = phases.astype(jnp.float32) * (2.0 * math.pi / samples)
    weights = jnp.stack([jnp.cos(angles), -jnp.sin(angles)], axis=1)
    return weights.reshape(2 * FREQS, samples) * (1.0 / math.sqrt(samples))

def reference(traces, sketch):
    sources, receivers, samples = traces.shape
    spectrum = lax.dot_general(dft_rows(samples), traces.reshape(sources * receivers, samples), (((1,), (1,)), ((), ())), precision=lax.Precision.HIGHEST)
    spectrum = spectrum.reshape(FREQS, 2, sources, receivers)
    symmetric = 0.5 * (spectrum + jnp.swapaxes(spectrum, 2, 3))
    sketched = jnp.einsum('fprn,nk->fprk', symmetric, sketch, precision=lax.Precision.HIGHEST)
    stacked = sketched.reshape(FREQS, 2 * sources, RANK)
    orth_q, upper_r = jnp.linalg.qr(stacked)
    diag_signs = jnp.sign(jnp.diagonal(upper_r, axis1=1, axis2=2))
    scaling = math.sqrt(2.0 * receivers)
    range_basis = (orth_q * diag_signs[:, None, :]).reshape(FREQS, 2, sources, RANK) * scaling
    r_factor = upper_r * diag_signs[:, :, None] / scaling
    return (range_basis, r_factor)
```

```python
import math

import jax
import jax.numpy as jnp
import numpy as np
from jax import lax
from jax.experimental import pallas as pl
from jax.experimental.pallas import tpu as pltpu
from jax.sharding import PartitionSpec as P

FREQS = 32
RANK = 64
F32 = jnp.float32
BF16 = jnp.bfloat16
NT = (((1,), (1,)), ((), ()))
NN = (((1,), (0,)), ((), ()))


def dft_rows(samples):
    times = np.arange(samples)
    orders = np.arange(1, FREQS + 1)
    angles = (orders[:, None] * times[None, :] % samples) * (2.0 * math.pi / samples)
    weights = np.stack([np.cos(angles), -np.sin(angles)], axis=1)
    return (weights.reshape(2 * FREQS, samples) / math.sqrt(samples)).astype(np.float32)


def split(x):
    high = x.astype(BF16)
    return high, (x - high.astype(F32)).astype(BF16)


def mm(a, b, dims):
    return lax.dot_general(a, b, dims, preferred_element_type=F32)


def low_lanes(shape):
    return lax.broadcasted_iota(jnp.int32, shape, 1) < 64


def dft_kernel(x_ref, w_ref, st_ref, spec_ref, d_ref):
    weights = w_ref[...]
    parts = [[None, None] for _ in range(4)]
    for tile in range(2):
        for half in range(2):
            x = x_ref[4 * half : 4 * half + 4, 64 * tile : 64 * tile + 64, :].reshape(256, -1)
            high, low = split(x)
            both = mm(weights, high, NT)
            out = both[:64] + both[64:] + mm(weights[:64], low, NT)
            for c in range(2):
                piece = out[:, 128 * c : 128 * c + 128]
                spec_ref[8 * tile : 8 * tile + 8, 2 * half + c] = piece.reshape(8, 8, 128)
                parts[2 * half + c][tile] = piece
    rows = jnp.concatenate([jnp.concatenate(p, axis=1) for p in parts], axis=0)
    st = st_ref[...]
    rolled = pltpu.roll(st, 64, 1)
    low_half = low_lanes(st.shape)
    zero = jnp.zeros_like(st)
    even = jnp.concatenate([jnp.where(low_half, st, zero), jnp.where(low_half, rolled, zero)], axis=1)
    odd = jnp.concatenate([jnp.where(low_half, zero, rolled), jnp.where(low_half, zero, st)], axis=1)
    s_high, s_low = split(jnp.concatenate([even, odd], axis=0))
    high, low = split(rows)
    both = mm(high, jnp.concatenate([s_high, s_low], axis=0), NT)
    out = both[:, :128] + both[:, 128:] + mm(low, s_high, NT)

    @pl.when(pl.program_id(0) == 0)
    def _():
        d_ref[...] = jnp.zeros_like(d_ref)

    for a in range(4):
        d_ref[:, a] += out[64 * a : 64 * a + 64].reshape(8, 8, 128)


def sketch_kernel(r_ref, d_ref, s_ref, gram_ref, z_ref, dn_ref):
    depth = r_ref.shape[0] // 8
    s_even = s_ref[pl.ds(0, depth, stride=2), :]
    s_odd = s_ref[pl.ds(1, depth, stride=2), :]
    s_high, s_low = split(jnp.transpose(jnp.concatenate([s_even, s_odd], axis=1)))
    s_both = jnp.concatenate([s_high, s_low], axis=0)
    low_half = low_lanes((64, 128))
    low_rows = low_lanes((32, 128))
    for q in range(2):
        halves = []
        for f in range(2):
            sums = []
            for p in range(2):
                part = 4 * q + 2 * f + p
                high, low = split(r_ref[pl.ds(part, depth, stride=8), :])
                both = mm(s_both, high, NN)
                sums.append(both[:128] + both[128:] + mm(s_high, low, NN))
            x, y = sums
            halves.append(
                jnp.where(
                    low_half,
                    x[:64] + pltpu.roll(x[64:], 64, 1),
                    pltpu.roll(y[:64], 64, 1) + y[64:],
                )
            )
        reverse = jnp.transpose(jnp.concatenate(halves, axis=0))
        for p in range(2):
            first = d_ref[pl.ds(4 * q + p, 32, stride=8), :]
            second = d_ref[pl.ds(4 * q + 2 + p, 32, stride=8), :]
            dn_ref[pl.ds(64 * p, 32, stride=2), :] = jnp.where(low_rows, first, pltpu.roll(second, 64, 1))
            dn_ref[pl.ds(64 * p + 1, 32, stride=2), :] = jnp.where(low_rows, pltpu.roll(first, 64, 1), second)
        z = 0.5 * (dn_ref[...] + reverse)
        z_ref[q] = z
        gram = lax.dot_general(z, z, (((0,), (0,)), ((), ())), precision=lax.Precision.HIGHEST, preferred_element_type=F32)
        gram_ref[q] = jnp.where(low_half, gram[:64], gram[64:])


def factor_kernel(scaling, g_ref, h_ref, z_ref, basis_ref, r_ref, u_ref, l_ref):
    lane = lax.broadcasted_iota(jnp.int32, (8, 128), 1)
    sub = lax.broadcasted_iota(jnp.int32, (8, 128), 0)
    base = lane - lane % 64
    inner = lane % 64
    g = [[g_ref[q, 8 * b : 8 * b + 8, :] + h_ref[q, 8 * b : 8 * b + 8, :] for b in range(8)] for q in range(2)]
    e = [[jnp.where(inner == sub + 8 * b, 1.0, 0.0).astype(F32) for b in range(8)] for q in range(2)]
    for j in range(64):
        top, row = j // 8, j % 8
        index = base + j
        for q in range(2):
            cols = {b: jnp.take_along_axis(g[q][b], index, axis=1) for b in range(top, 8)}
            pivot = jnp.broadcast_to(cols[top][row : row + 1], (8, 128))
            grow = jnp.broadcast_to(g[q][top][row : row + 1], (8, 128))
            erow = jnp.broadcast_to(e[q][top][row : row + 1], (8, 128))
            scale = lax.rsqrt(pivot)
            scale = scale * (1.5 - 0.5 * pivot * scale * scale)
            u_ref[q, j : j + 1, :] = jnp.where(inner >= j, grow * scale, 0.0)[:1]
            l_ref[q, j : j + 1, :] = (erow * scale)[:1]
            inverse = 1.0 / pivot
            grow = grow * inverse
            erow = erow * inverse
            for b in range(top, 8):
                c = cols[b]
                if b == top:
                    c = jnp.where(sub > row, c, 0.0)
                g[q][b] = g[q][b] - c * grow
                e[q][b] = e[q][b] - c * erow
    low_half = low_lanes((64, 128))
    for q in range(2):
        u = u_ref[q] * (1.0 / scaling)
        r_ref[2 * q] = u[:, :64]
        r_ref[2 * q + 1] = pltpu.roll(u, 64, 1)[:, :64]
        inv = l_ref[q]
        inv = jnp.concatenate([jnp.where(low_half, inv, 0.0), jnp.where(low_half, 0.0, inv)], axis=0)
        out = lax.dot_general(z_ref[q], inv, NT, precision=lax.Precision.HIGHEST, preferred_element_type=F32) * scaling
        turned = pltpu.roll(out, 64, 1)
        for p in range(2):
            basis_ref[2 * q, p] = out[64 * p : 64 * p + 64, :64]
            basis_ref[2 * q + 1, p] = turned[64 * p : 64 * p + 64, :64]


def local(traces, sketch):
    shots, receivers, samples = traces.shape
    devices = lax.axis_size("src") * lax.axis_size("rcv")
    rcv_count = lax.axis_size("rcv")
    weights = dft_rows(samples)
    w_high = weights.astype(BF16)
    w_low = (weights - w_high.astype(np.float32)).astype(BF16)
    w_both = jnp.asarray(np.concatenate([w_high, w_low], axis=0))
    sd = jax.ShapeDtypeStruct
    spec, own = pl.pallas_call(
        dft_kernel,
        grid=(receivers // 128,),
        in_specs=[
            pl.BlockSpec((shots, 128, samples), lambda g: (0, g, 0)),
            pl.BlockSpec((128, samples), lambda g: (0, 0)),
            pl.BlockSpec((RANK, 128), lambda g: (0, g)),
        ],
        out_specs=[
            pl.BlockSpec((16, 4, 8, 128), lambda g: (g, 0, 0, 0)),
            pl.BlockSpec((rcv_count, 4, 8, 128), lambda g: (0, 0, 0, 0)),
        ],
        out_shape=[sd((devices, 4, 8, 128), F32), sd((rcv_count, 4, 8, 128), F32)],
        name="dft",
    )(traces, w_both, sketch.T)
    direct = lax.all_to_all(own.reshape(rcv_count, 32, 128), "rcv", split_axis=0, concat_axis=0, tiled=True)
    received = lax.all_to_all(spec.reshape(devices, 32, 128), ("src", "rcv"), split_axis=0, concat_axis=0, tiled=True)
    gram, z = pl.pallas_call(
        sketch_kernel,
        out_shape=[sd((2, 64, 128), F32), sd((2, 128, 128), F32)],
        scratch_shapes=[pltpu.VMEM((128, 128), F32)],
        name="sketch",
    )(received.reshape(devices * 32, 128), direct.reshape(rcv_count * 32, 128), sketch)
    src = lax.axis_size("src")
    for bits in (1, 8, 2):
        gram = gram + lax.ppermute(gram, "src", [(s, s ^ bits) for s in range(src)])
    other = lax.ppermute(gram, "src", [(s, s ^ 6) for s in range(src)])
    scaling = math.sqrt(2.0 * receivers)
    basis, r_factor = pl.pallas_call(
        lambda *refs: factor_kernel(scaling, *refs),
        out_shape=[sd((4, 2, 64, 64), F32), sd((4, 64, 64), F32)],
        scratch_shapes=[pltpu.VMEM((2, 64, 128), F32), pltpu.VMEM((2, 64, 128), F32)],
        name="factor",
    )(gram, other, z)
    return basis, r_factor


def solution(mesh):
    in_specs = (P(("src", "rcv"), None, None), P())
    out_specs = (P("rcv", None, "src", None), P("rcv", None, None))
    return jax.shard_map(local, mesh=mesh, in_specs=in_specs, out_specs=out_specs, check_vma=False)
```

```python
import math

import jax
import jax.numpy as jnp
import numpy as np
from jax import lax
from jax.experimental import pallas as pl
from jax.experimental.pallas import tpu as pltpu
from jax.sharding import PartitionSpec as P


FREQS = 32
RANK = 64
F32 = jnp.float32
BF16 = jnp.bfloat16
NT = (((1,), (1,)), ((), ()))
NN = (((1,), (0,)), ((), ()))


def dft_rows(samples):
    times = np.arange(samples)
    orders = np.arange(1, FREQS + 1)
    angles = (orders[:, None] * times[None, :] % samples) * (2.0 * math.pi / samples)
    weights = np.stack([np.cos(angles), -np.sin(angles)], axis=1)
    return (weights.reshape(2 * FREQS, samples) / math.sqrt(samples)).astype(np.float32)


def small(mib):
    return dict(compiler_params=pltpu.CompilerParams(vmem_limit_bytes=mib << 20))


def split(x):
    high = x.astype(BF16)
    return high, (x - high.astype(F32)).astype(BF16)


def mm(a, b, dims):
    return lax.dot_general(a, b, dims, preferred_element_type=F32)


def low_lanes(shape):
    return lax.broadcasted_iota(jnp.int32, shape, 1) < 64


def dft_kernel(x_hbm, w_hbm, spec_hbm, x_ref, w_ref, out_ref, x_sems, w_sem, out_sems):
    steps = x_ref.shape[1] // 128
    ahead = 3

    def fetch(step):
        span = pl.ds(pl.multiple_of(128 * step, 128), 128)
        return pltpu.make_async_copy(x_hbm.at[:, span, :], x_ref.at[:, span, :], x_sems.at[step])

    def put(step):
        span = pl.ds(pl.multiple_of(16 * step, 16), 16)
        return pltpu.make_async_copy(out_ref.at[span], spec_hbm.at[span], out_sems.at[step])

    w_copy = pltpu.make_async_copy(w_hbm, w_ref, w_sem)
    w_copy.start()
    for step in range(ahead):
        fetch(step).start()
    w_copy.wait()

    def body(step, carry):
        fetch(step).wait()

        @pl.when(step + ahead < steps)
        def _():
            fetch(step + ahead).start()

        weights = w_ref[...]
        for tile in range(2):
            rows = pl.ds(pl.multiple_of(128 * step + 64 * tile, 64), 64)
            dest = pl.ds(pl.multiple_of(16 * step + 8 * tile, 8), 8)
            for half in range(2):
                high, low = split(x_ref[4 * half : 4 * half + 4, rows, :].reshape(256, -1))
                both = mm(weights, high, NT)
                out = both[:64] + both[64:] + mm(weights[:64], low, NT)
                for c in range(2):
                    out_ref[dest, 2 * half + c] = out[:, 128 * c : 128 * c + 128].reshape(8, 8, 128)
        put(step).start()
        return carry

    lax.fori_loop(0, steps, body, 0)
    for step in range(steps):
        put(step).wait()


def own_kernel(spec_ref, st_ref, *refs):
    d_ref = refs[-1]
    low_half = low_lanes((64, 128))
    zero = jnp.zeros((64, 128), F32)
    total = None
    for g in range(spec_ref.shape[0] // 16):
        rows = jnp.concatenate(
            [
                jnp.concatenate(
                    [spec_ref[16 * g + 8 * t : 16 * g + 8 * t + 8, a].reshape(64, 128) for t in range(2)], axis=1
                )
                for a in range(4)
            ],
            axis=0,
        )
        st = st_ref[:, 128 * g : 128 * g + 128]
        rolled = pltpu.roll(st, 64, 1)
        even = jnp.concatenate([jnp.where(low_half, st, zero), jnp.where(low_half, rolled, zero)], axis=1)
        odd = jnp.concatenate([jnp.where(low_half, zero, rolled), jnp.where(low_half, zero, st)], axis=1)
        s_high, s_low = split(jnp.concatenate([even, odd], axis=0))
        high, low = split(rows)
        both = mm(high, jnp.concatenate([s_high, s_low], axis=0), NT)
        out = both[:, :128] + both[:, 128:] + mm(low, s_high, NT)
        total = out if total is None else total + out

    @pl.when(pl.program_id(0) == 0)
    def _():
        d_ref[...] = jnp.zeros_like(d_ref)

    for a in range(4):
        d_ref[:, a] += total[64 * a : 64 * a + 64].reshape(8, 8, 128)

    @pl.when(pl.program_id(0) == pl.num_programs(0) - 1)
    def _():
        me = lax.axis_index("rcv")
        for slot, ref in enumerate(refs[:-1]):
            ref[...] = d_ref[slot ^ me]


def place_kernel(*refs):
    out_ref = refs[-1]
    me = lax.axis_index("rcv")
    low_half = low_lanes((4, 128))
    for slot, ref in enumerate(refs[:-1]):
        row = pl.multiple_of(8 * (slot ^ me), 8)
        for q in range(2):
            for p in range(2):
                first, second = ref[:, 4 * q + p, :], ref[:, 4 * q + 2 + p, :]
                even = jnp.where(low_half, first, pltpu.roll(second, 64, 1))
                odd = jnp.where(low_half, pltpu.roll(first, 64, 1), second)
                for a in range(4):
                    out_ref[q, pl.ds(64 * p + row + 2 * a, 1), :] = even[a : a + 1]
                    out_ref[q, pl.ds(64 * p + row + 2 * a + 1, 1), :] = odd[a : a + 1]


def sketch_kernel(r_ref, d_ref, s_ref, gram_ref, z_ref, acc_ref):
    step = pl.program_id(0)
    depth = r_ref.shape[0] // 8
    s_even = s_ref[pl.ds(0, depth, stride=2), :]
    s_odd = s_ref[pl.ds(1, depth, stride=2), :]
    s_high, s_low = split(jnp.transpose(jnp.concatenate([s_even, s_odd], axis=1)))
    s_both = jnp.concatenate([s_high, s_low], axis=0)

    @pl.when(step == 0)
    def _():
        acc_ref[...] = jnp.zeros_like(acc_ref)

    for pair in range(4):
        block = jnp.concatenate([r_ref[pl.ds(2 * pair + p, depth, stride=8), :] for p in range(2)], axis=1)
        high, low = split(block)
        both = mm(s_both, high, NN)
        acc_ref[pair] += both[:128] + both[128:] + mm(s_high, low, NN)

    @pl.when(step == pl.num_programs(0) - 1)
    def _():
        low_half = low_lanes((64, 128))
        for q in range(2):
            halves = []
            for f in range(2):
                sums = acc_ref[2 * q + f]
                x, y = sums[:, :128], sums[:, 128:]
                halves.append(
                    jnp.where(
                        low_half,
                        x[:64] + pltpu.roll(x[64:], 64, 1),
                        pltpu.roll(y[:64], 64, 1) + y[64:],
                    )
                )
            reverse = jnp.transpose(jnp.concatenate(halves, axis=0))
            z = 0.5 * (d_ref[q] + reverse)
            z_ref[q] = z
            gram = lax.dot_general(
                z, z, (((0,), (0,)), ((), ())), precision=lax.Precision.HIGHEST, preferred_element_type=F32
            )
            gram_ref[q] = jnp.where(low_half, gram[:64], gram[64:])


def factor_kernel(scaling, g_ref, h_ref, z_ref, basis_ref, r_ref, u_ref, l_ref):
    lane = lax.broadcasted_iota(jnp.int32, (8, 128), 1)
    sub = lax.broadcasted_iota(jnp.int32, (8, 128), 0)
    base = lane - lane % 64
    inner = lane % 64
    g = [[g_ref[q, 8 * b : 8 * b + 8, :] + h_ref[q, 8 * b : 8 * b + 8, :] for b in range(8)] for q in range(2)]
    e = [[jnp.where(inner == sub + 8 * b, 1.0, 0.0).astype(F32) for b in range(8)] for _ in range(2)]
    for j in range(64):
        top, row = j // 8, j % 8
        index = base + j
        for q in range(2):
            cols = {b: jnp.take_along_axis(g[q][b], index, axis=1) for b in range(top, 8)}
            pivot = jnp.broadcast_to(cols[top][row : row + 1], (8, 128))
            grow = jnp.broadcast_to(g[q][top][row : row + 1], (8, 128))
            erow = jnp.broadcast_to(e[q][top][row : row + 1], (8, 128))
            scale = lax.rsqrt(pivot)
            scale = scale * (1.5 - 0.5 * pivot * scale * scale)
            u_ref[q, j : j + 1, :] = jnp.where(inner >= j, grow * scale, 0.0)[:1]
            l_ref[q, j : j + 1, :] = (erow * scale)[:1]
            inverse = 1.0 / pivot
            grow = grow * inverse
            erow = erow * inverse
            for b in range(top, 8):
                c = cols[b]
                if b == top:
                    c = jnp.where(sub > row, c, 0.0)
                g[q][b] = g[q][b] - c * grow
                e[q][b] = e[q][b] - c * erow
    low_half = low_lanes((64, 128))
    for q in range(2):
        u = u_ref[q] * (1.0 / scaling)
        r_ref[2 * q] = u[:, :64]
        r_ref[2 * q + 1] = pltpu.roll(u, 64, 1)[:, :64]
        inv = l_ref[q]
        inv = jnp.concatenate([jnp.where(low_half, inv, 0.0), jnp.where(low_half, 0.0, inv)], axis=0)
        out = lax.dot_general(z_ref[q], inv, NT, precision=lax.Precision.HIGHEST, preferred_element_type=F32) * scaling
        turned = pltpu.roll(out, 64, 1)
        for p in range(2):
            basis_ref[2 * q, p] = out[64 * p : 64 * p + 64, :64]
            basis_ref[2 * q + 1, p] = turned[64 * p : 64 * p + 64, :64]


def local(traces, sketch):
    shots, receivers, samples = traces.shape
    devices = lax.axis_size("src") * lax.axis_size("rcv")
    rcv_count = lax.axis_size("rcv")
    weights = dft_rows(samples)
    w_high = weights.astype(BF16)
    w_low = (weights - w_high.astype(np.float32)).astype(BF16)
    w_both = jnp.asarray(np.concatenate([w_high, w_low], axis=0))
    sd = jax.ShapeDtypeStruct
    spec = pl.pallas_call(
        dft_kernel,
        in_specs=[pl.BlockSpec(memory_space=pltpu.HBM)] * 2,
        out_specs=pl.BlockSpec(memory_space=pltpu.HBM),
        out_shape=sd((devices, 4, 8, 128), F32),
        scratch_shapes=[
            pltpu.VMEM((shots, receivers, samples), F32),
            pltpu.VMEM((128, samples), BF16),
            pltpu.VMEM((devices, 4, 8, 128), F32),
            pltpu.SemaphoreType.DMA((receivers // 128,)),
            pltpu.SemaphoreType.DMA,
            pltpu.SemaphoreType.DMA((receivers // 128,)),
        ],
        cost_estimate=pl.CostEstimate(flops=3 * 2 * 64 * 8192 * 512, bytes_accessed=19 << 20, transcendentals=0),
        name="dft",
    )(traces, w_both)
    received = lax.all_to_all(spec.reshape(devices, 32, 128), ("src", "rcv"), split_axis=0, concat_axis=0, tiled=True)
    own = pl.pallas_call(
        own_kernel,
        grid=(2,),
        in_specs=[
            pl.BlockSpec((devices // 2, 4, 8, 128), lambda g: (g, 0, 0, 0)),
            pl.BlockSpec((RANK, receivers // 2), lambda g: (0, g)),
        ],
        out_specs=[pl.BlockSpec((4, 8, 128), lambda g: (0, 0, 0))] * rcv_count,
        out_shape=[sd((4, 8, 128), F32)] * rcv_count,
        scratch_shapes=[pltpu.VMEM((rcv_count, 4, 8, 128), F32)],
        cost_estimate=pl.CostEstimate(flops=3 << 30, bytes_accessed=4 << 20, transcendentals=0),
        name="own",
        **small(8),
    )
    pieces = list(own(pltpu.with_memory_space_constraint(spec, pltpu.HBM), sketch.T))
    for slot in range(1, rcv_count):
        pairs = [(r, r ^ slot) for r in range(rcv_count)]
        pieces[slot] = lax.ppermute(pieces[slot], "rcv", pairs)
    direct = pl.pallas_call(place_kernel, out_shape=sd((2, 128, 128), F32), name="place", **small(8))(*pieces)
    gram, z = pl.pallas_call(
        sketch_kernel,
        grid=(2,),
        in_specs=[
            pl.BlockSpec((devices * 16, 128), lambda g: (g, 0)),
            pl.BlockSpec((2, 128, 128), lambda g: (0, 0, 0)),
            pl.BlockSpec((receivers // 2, RANK), lambda g: (g, 0)),
        ],
        out_specs=[pl.BlockSpec((2, 64, 128), lambda g: (0, 0, 0)), pl.BlockSpec((2, 128, 128), lambda g: (0, 0, 0))],
        out_shape=[sd((2, 64, 128), F32), sd((2, 128, 128), F32)],
        scratch_shapes=[pltpu.VMEM((4, 128, 256), F32)],
        name="sketch",
        **small(12),
    )(pltpu.with_memory_space_constraint(received.reshape(devices * 32, 128), pltpu.VMEM), direct, sketch)
    src = lax.axis_size("src")
    for bits in (1, 8, 2):
        gram = gram + lax.ppermute(gram, "src", [(s, s ^ bits) for s in range(src)])
    other = lax.ppermute(gram, "src", [(s, s ^ 6) for s in range(src)])
    scaling = math.sqrt(2.0 * receivers)
    basis, r_factor = pl.pallas_call(
        lambda *refs: factor_kernel(scaling, *refs),
        out_shape=[sd((4, 2, 64, 64), F32), sd((4, 64, 64), F32)],
        scratch_shapes=[pltpu.VMEM((2, 64, 128), F32), pltpu.VMEM((2, 64, 128), F32)],
        name="factor",
        **small(8),
    )(gram, other, z)
    return basis, r_factor


def solution(mesh):
    in_specs = (P(("src", "rcv"), None, None), P())
    out_specs = (P("rcv", None, "src", None), P("rcv", None, None))
    return jax.shard_map(local, mesh=mesh, in_specs=in_specs, out_specs=out_specs, check_vma=False)
```

```python
import math

import jax
import jax.numpy as jnp
import numpy as np
from jax import lax
from jax.experimental import pallas as pl
from jax.experimental.pallas import tpu as pltpu
from jax.sharding import PartitionSpec as P


FREQS = 32
RANK = 64
F32 = jnp.float32
BF16 = jnp.bfloat16
NT = (((1,), (1,)), ((), ()))
NN = (((1,), (0,)), ((), ()))


def dft_rows(samples):
    times = np.arange(samples)
    orders = np.arange(1, FREQS + 1)
    angles = (orders[:, None] * times[None, :] % samples) * (2.0 * math.pi / samples)
    weights = np.stack([np.cos(angles), -np.sin(angles)], axis=1)
    return (weights.reshape(2 * FREQS, samples) / math.sqrt(samples)).astype(np.float32)


def small(mib):
    return dict(compiler_params=pltpu.CompilerParams(vmem_limit_bytes=mib << 20))


def split(x):
    high = x.astype(BF16)
    return high, (x - high.astype(F32)).astype(BF16)


def mm(a, b, dims):
    return lax.dot_general(a, b, dims, preferred_element_type=F32)


def low_lanes(shape):
    return lax.broadcasted_iota(jnp.int32, shape, 1) < 64


def dft_kernel(x_hbm, w_hbm, spec_hbm, x_ref, w_ref, out_ref, x_sems, w_sem, out_sems):
    steps = x_ref.shape[1] // 128
    ahead = 3

    def fetch(step):
        span = pl.ds(pl.multiple_of(128 * step, 128), 128)
        return pltpu.make_async_copy(x_hbm.at[:, span, :], x_ref.at[:, span, :], x_sems.at[step])

    def put(step):
        span = pl.ds(pl.multiple_of(16 * step, 16), 16)
        return pltpu.make_async_copy(out_ref.at[span], spec_hbm.at[span], out_sems.at[step])

    w_copy = pltpu.make_async_copy(w_hbm, w_ref, w_sem)
    w_copy.start()
    for step in range(ahead):
        fetch(step).start()
    w_copy.wait()

    def body(step, carry):
        fetch(step).wait()

        @pl.when(step + ahead < steps)
        def _():
            fetch(step + ahead).start()

        weights = w_ref[...]
        for tile in range(2):
            rows = pl.ds(pl.multiple_of(128 * step + 64 * tile, 64), 64)
            dest = pl.ds(pl.multiple_of(16 * step + 8 * tile, 8), 8)
            for half in range(2):
                high, low = split(x_ref[4 * half : 4 * half + 4, rows, :].reshape(256, -1))
                both = mm(weights, high, NT)
                out = both[:64] + both[64:] + mm(weights[:64], low, NT)
                for c in range(2):
                    out_ref[dest, 2 * half + c] = out[:, 128 * c : 128 * c + 128].reshape(8, 8, 128)
        put(step).start()
        return carry

    lax.fori_loop(0, steps, body, 0)
    for step in range(steps):
        put(step).wait()


def own_kernel(spec_ref, st_ref, *refs):
    d_ref = refs[-1]
    low_half = low_lanes((64, 128))
    zero = jnp.zeros((64, 128), F32)
    total = None
    for g in range(spec_ref.shape[0] // 16):
        rows = jnp.concatenate(
            [
                jnp.concatenate(
                    [spec_ref[16 * g + 8 * t : 16 * g + 8 * t + 8, a].reshape(64, 128) for t in range(2)], axis=1
                )
                for a in range(4)
            ],
            axis=0,
        )
        st = st_ref[:, 128 * g : 128 * g + 128]
        rolled = pltpu.roll(st, 64, 1)
        even = jnp.concatenate([jnp.where(low_half, st, zero), jnp.where(low_half, rolled, zero)], axis=1)
        odd = jnp.concatenate([jnp.where(low_half, zero, rolled), jnp.where(low_half, zero, st)], axis=1)
        s_high, s_low = split(jnp.concatenate([even, odd], axis=0))
        high, low = split(rows)
        both = mm(high, jnp.concatenate([s_high, s_low], axis=0), NT)
        out = both[:, :128] + both[:, 128:] + mm(low, s_high, NT)
        total = out if total is None else total + out

    @pl.when(pl.program_id(0) == 0)
    def _():
        d_ref[...] = jnp.zeros_like(d_ref)

    for a in range(4):
        d_ref[:, a] += total[64 * a : 64 * a + 64].reshape(8, 8, 128)

    @pl.when(pl.program_id(0) == pl.num_programs(0) - 1)
    def _():
        me = lax.axis_index("rcv")
        for slot, ref in enumerate(refs[:-1]):
            ref[...] = d_ref[slot ^ me]


def place_kernel(*refs):
    out_ref = refs[-1]
    me = lax.axis_index("rcv")
    low_half = low_lanes((4, 128))
    for slot, ref in enumerate(refs[:-1]):
        row = pl.multiple_of(8 * (slot ^ me), 8)
        for q in range(2):
            for p in range(2):
                first, second = ref[:, 4 * q + p, :], ref[:, 4 * q + 2 + p, :]
                even = jnp.where(low_half, first, pltpu.roll(second, 64, 1))
                odd = jnp.where(low_half, pltpu.roll(first, 64, 1), second)
                for a in range(4):
                    out_ref[q, pl.ds(64 * p + row + 2 * a, 1), :] = even[a : a + 1]
                    out_ref[q, pl.ds(64 * p + row + 2 * a + 1, 1), :] = odd[a : a + 1]


def sketch_kernel(r_ref, d_ref, s_ref, gram_ref, z_ref, acc_ref):
    step = pl.program_id(0)
    depth = r_ref.shape[0] // 8
    s_even = s_ref[pl.ds(0, depth, stride=2), :]
    s_odd = s_ref[pl.ds(1, depth, stride=2), :]
    s_high, s_low = split(jnp.transpose(jnp.concatenate([s_even, s_odd], axis=1)))
    s_both = jnp.concatenate([s_high, s_low], axis=0)

    @pl.when(step == 0)
    def _():
        acc_ref[...] = jnp.zeros_like(acc_ref)

    for pair in range(4):
        block = jnp.concatenate([r_ref[pl.ds(2 * pair + p, depth, stride=8), :] for p in range(2)], axis=1)
        high, low = split(block)
        both = mm(s_both, high, NN)
        acc_ref[pair] += both[:128] + both[128:] + mm(s_high, low, NN)

    @pl.when(step == pl.num_programs(0) - 1)
    def _():
        low_half = low_lanes((64, 128))
        for q in range(2):
            halves = []
            for f in range(2):
                sums = acc_ref[2 * q + f]
                x, y = sums[:, :128], sums[:, 128:]
                halves.append(
                    jnp.where(
                        low_half,
                        x[:64] + pltpu.roll(x[64:], 64, 1),
                        pltpu.roll(y[:64], 64, 1) + y[64:],
                    )
                )
            reverse = jnp.transpose(jnp.concatenate(halves, axis=0))
            z = 0.5 * (d_ref[q] + reverse)
            z_ref[q] = z
            gram = lax.dot_general(
                z, z, (((0,), (0,)), ((), ())), precision=lax.Precision.HIGHEST, preferred_element_type=F32
            )
            gram_ref[q] = jnp.where(low_half, gram[:64], gram[64:])


def factor_kernel(scaling, g_ref, h_ref, z_ref, basis_ref, r_ref, u_ref, l_ref):
    lane = lax.broadcasted_iota(jnp.int32, (8, 128), 1)
    sub = lax.broadcasted_iota(jnp.int32, (8, 128), 0)
    base = lane - lane % 64
    inner = lane % 64
    g = [[g_ref[q, 8 * b : 8 * b + 8, :] + h_ref[q, 8 * b : 8 * b + 8, :] for b in range(8)] for q in range(2)]
    e = [[jnp.where(inner == sub + 8 * b, 1.0, 0.0).astype(F32) for b in range(8)] for _ in range(2)]

    def spread(x, row):
        return jnp.broadcast_to(x[row : row + 1], (8, 128))

    for top in range(8):
        cols = [
            [[jnp.take_along_axis(g[q][b], base + (8 * top + a), axis=1) for b in range(top, 8)] for a in range(8)]
            for q in range(2)
        ]
        for a in range(8):
            j = 8 * top + a
            for q in range(2):
                pivot = spread(cols[q][a][0], a)
                inverse = 1.0 / pivot
                mult = [x * inverse for x in cols[q][a]]
                for later in range(a + 1, 8):
                    weight = spread(cols[q][later][0], a)
                    cols[q][later] = [x - m * weight for x, m in zip(cols[q][later], mult)]
                grow = spread(g[q][top], a)
                erow = spread(e[q][top], a)
                scale = lax.rsqrt(pivot)
                scale = scale * (1.5 - 0.5 * pivot * scale * scale)
                u_ref[q, j : j + 1, :] = jnp.where(inner >= j, grow * scale, 0.0)[:1]
                l_ref[q, j : j + 1, :] = (erow * scale)[:1]
                mult[0] = jnp.where(sub > a, mult[0], 0.0)
                for b in range(top, 8):
                    g[q][b] = g[q][b] - mult[b - top] * grow
                    e[q][b] = e[q][b] - mult[b - top] * erow
    low_half = low_lanes((64, 128))
    for q in range(2):
        u = u_ref[q] * (1.0 / scaling)
        r_ref[2 * q] = u[:, :64]
        r_ref[2 * q + 1] = pltpu.roll(u, 64, 1)[:, :64]
        inv = l_ref[q]
        inv = jnp.concatenate([jnp.where(low_half, inv, 0.0), jnp.where(low_half, 0.0, inv)], axis=0)
        out = lax.dot_general(z_ref[q], inv, NT, precision=lax.Precision.HIGHEST, preferred_element_type=F32) * scaling
        turned = pltpu.roll(out, 64, 1)
        for p in range(2):
            basis_ref[2 * q, p] = out[64 * p : 64 * p + 64, :64]
            basis_ref[2 * q + 1, p] = turned[64 * p : 64 * p + 64, :64]


def local(traces, sketch):
    shots, receivers, samples = traces.shape
    devices = lax.axis_size("src") * lax.axis_size("rcv")
    rcv_count = lax.axis_size("rcv")
    weights = dft_rows(samples)
    w_high = weights.astype(BF16)
    w_low = (weights - w_high.astype(np.float32)).astype(BF16)
    w_both = jnp.asarray(np.concatenate([w_high, w_low], axis=0))
    sd = jax.ShapeDtypeStruct
    spec = pl.pallas_call(
        dft_kernel,
        in_specs=[pl.BlockSpec(memory_space=pltpu.HBM)] * 2,
        out_specs=pl.BlockSpec(memory_space=pltpu.HBM),
        out_shape=sd((devices, 4, 8, 128), F32),
        scratch_shapes=[
            pltpu.VMEM((shots, receivers, samples), F32),
            pltpu.VMEM((128, samples), BF16),
            pltpu.VMEM((devices, 4, 8, 128), F32),
            pltpu.SemaphoreType.DMA((receivers // 128,)),
            pltpu.SemaphoreType.DMA,
            pltpu.SemaphoreType.DMA((receivers // 128,)),
        ],
        cost_estimate=pl.CostEstimate(flops=3 * 2 * 64 * 8192 * 512, bytes_accessed=19 << 20, transcendentals=0),
        name="dft",
    )(traces, w_both)
    received = lax.all_to_all(spec.reshape(devices, 32, 128), ("src", "rcv"), split_axis=0, concat_axis=0, tiled=True)
    own = pl.pallas_call(
        own_kernel,
        grid=(2,),
        in_specs=[
            pl.BlockSpec((devices // 2, 4, 8, 128), lambda g: (g, 0, 0, 0)),
            pl.BlockSpec((RANK, receivers // 2), lambda g: (0, g)),
        ],
        out_specs=[pl.BlockSpec((4, 8, 128), lambda g: (0, 0, 0))] * rcv_count,
        out_shape=[sd((4, 8, 128), F32)] * rcv_count,
        scratch_shapes=[pltpu.VMEM((rcv_count, 4, 8, 128), F32)],
        cost_estimate=pl.CostEstimate(flops=3 << 30, bytes_accessed=4 << 20, transcendentals=0),
        name="own",
        **small(8),
    )
    pieces = list(own(pltpu.with_memory_space_constraint(spec, pltpu.HBM), sketch.T))
    for slot in range(1, rcv_count):
        pairs = [(r, r ^ slot) for r in range(rcv_count)]
        pieces[slot] = lax.ppermute(pieces[slot], "rcv", pairs)
    direct = pl.pallas_call(place_kernel, out_shape=sd((2, 128, 128), F32), name="place", **small(8))(*pieces)
    gram, z = pl.pallas_call(
        sketch_kernel,
        grid=(2,),
        in_specs=[
            pl.BlockSpec((devices * 16, 128), lambda g: (g, 0)),
            pl.BlockSpec((2, 128, 128), lambda g: (0, 0, 0)),
            pl.BlockSpec((receivers // 2, RANK), lambda g: (g, 0)),
        ],
        out_specs=[pl.BlockSpec((2, 64, 128), lambda g: (0, 0, 0)), pl.BlockSpec((2, 128, 128), lambda g: (0, 0, 0))],
        out_shape=[sd((2, 64, 128), F32), sd((2, 128, 128), F32)],
        scratch_shapes=[pltpu.VMEM((4, 128, 256), F32)],
        name="sketch",
        **small(12),
    )(pltpu.with_memory_space_constraint(received.reshape(devices * 32, 128), pltpu.VMEM), direct, sketch)
    src = lax.axis_size("src")
    for bits in (1, 8, 2):
        gram = gram + lax.ppermute(gram, "src", [(s, s ^ bits) for s in range(src)])
    other = lax.ppermute(gram, "src", [(s, s ^ 6) for s in range(src)])
    scaling = math.sqrt(2.0 * receivers)
    basis, r_factor = pl.pallas_call(
        lambda *refs: factor_kernel(scaling, *refs),
        out_shape=[sd((4, 2, 64, 64), F32), sd((4, 64, 64), F32)],
        scratch_shapes=[pltpu.VMEM((2, 64, 128), F32), pltpu.VMEM((2, 64, 128), F32)],
        name="factor",
        **small(8),
    )(gram, other, z)
    return basis, r_factor


def solution(mesh):
    in_specs = (P(("src", "rcv"), None, None), P())
    out_specs = (P("rcv", None, "src", None), P("rcv", None, None))
    return jax.shard_map(local, mesh=mesh, in_specs=in_specs, out_specs=out_specs, check_vma=False)
```

```python
import math

import jax
import jax.numpy as jnp
import numpy as np
from jax import lax
from jax.experimental import pallas as pl
from jax.experimental.pallas import tpu as pltpu
from jax.sharding import PartitionSpec as P


FREQS = 32
RANK = 64
F32 = jnp.float32
BF16 = jnp.bfloat16
NT = (((1,), (1,)), ((), ()))
NN = (((1,), (0,)), ((), ()))


def dft_rows(samples):
    times = np.arange(samples)
    orders = np.arange(1, FREQS + 1)
    angles = (orders[:, None] * times[None, :] % samples) * (2.0 * math.pi / samples)
    weights = np.stack([np.cos(angles), -np.sin(angles)], axis=1)
    return (weights.reshape(2 * FREQS, samples) / math.sqrt(samples)).astype(np.float32)


def small(mib):
    return dict(compiler_params=pltpu.CompilerParams(vmem_limit_bytes=mib << 20))


def split(x):
    high = x.astype(BF16)
    return high, (x - high.astype(F32)).astype(BF16)


def mm(a, b, dims):
    return lax.dot_general(a, b, dims, preferred_element_type=F32)


def low_lanes(shape):
    return lax.broadcasted_iota(jnp.int32, shape, 1) < 64


def dft_kernel(x_hbm, w_hbm, spec_hbm, x_ref, w_ref, out_ref, x_sems, w_sem, out_sems):
    steps = x_ref.shape[1] // 128
    ahead = 3

    def fetch(step):
        span = pl.ds(pl.multiple_of(128 * step, 128), 128)
        return pltpu.make_async_copy(x_hbm.at[:, span, :], x_ref.at[:, span, :], x_sems.at[step])

    def put(step):
        span = pl.ds(pl.multiple_of(16 * step, 16), 16)
        return pltpu.make_async_copy(out_ref.at[span], spec_hbm.at[span], out_sems.at[step])

    w_copy = pltpu.make_async_copy(w_hbm, w_ref, w_sem)
    w_copy.start()
    for step in range(ahead):
        fetch(step).start()
    w_copy.wait()

    def body(step, carry):
        fetch(step).wait()

        @pl.when(step + ahead < steps)
        def _():
            fetch(step + ahead).start()

        weights = w_ref[...]
        for tile in range(2):
            rows = pl.ds(pl.multiple_of(128 * step + 64 * tile, 64), 64)
            dest = pl.ds(pl.multiple_of(16 * step + 8 * tile, 8), 8)
            for half in range(2):
                high, low = split(x_ref[4 * half : 4 * half + 4, rows, :].reshape(256, -1))
                both = mm(weights, high, NT)
                out = both[:64] + both[64:] + mm(weights[:64], low, NT)
                for c in range(2):
                    out_ref[dest, 2 * half + c] = out[:, 128 * c : 128 * c + 128].reshape(8, 8, 128)
        put(step).start()
        return carry

    lax.fori_loop(0, steps, body, 0)
    for step in range(steps):
        put(step).wait()


def own_kernel(spec_ref, st_ref, *refs):
    d_ref = refs[-1]
    low_half = low_lanes((64, 128))
    zero = jnp.zeros((64, 128), F32)
    total = None
    for g in range(spec_ref.shape[0] // 16):
        rows = jnp.concatenate(
            [
                jnp.concatenate(
                    [spec_ref[16 * g + 8 * t : 16 * g + 8 * t + 8, a].reshape(64, 128) for t in range(2)], axis=1
                )
                for a in range(4)
            ],
            axis=0,
        )
        st = st_ref[:, 128 * g : 128 * g + 128]
        rolled = pltpu.roll(st, 64, 1)
        even = jnp.concatenate([jnp.where(low_half, st, zero), jnp.where(low_half, rolled, zero)], axis=1)
        odd = jnp.concatenate([jnp.where(low_half, zero, rolled), jnp.where(low_half, zero, st)], axis=1)
        s_high, s_low = split(jnp.concatenate([even, odd], axis=0))
        high, low = split(rows)
        both = mm(high, jnp.concatenate([s_high, s_low], axis=0), NT)
        out = both[:, :128] + both[:, 128:] + mm(low, s_high, NT)
        total = out if total is None else total + out

    @pl.when(pl.program_id(0) == 0)
    def _():
        d_ref[...] = jnp.zeros_like(d_ref)

    for a in range(4):
        d_ref[:, a] += total[64 * a : 64 * a + 64].reshape(8, 8, 128)

    @pl.when(pl.program_id(0) == pl.num_programs(0) - 1)
    def _():
        me = lax.axis_index("rcv")
        for slot, ref in enumerate(refs[:-1]):
            ref[...] = d_ref[slot ^ me]


def place_kernel(*refs):
    out_ref = refs[-1]
    me = lax.axis_index("rcv")
    low_half = low_lanes((4, 128))
    for slot, ref in enumerate(refs[:-1]):
        row = pl.multiple_of(8 * (slot ^ me), 8)
        for q in range(2):
            for p in range(2):
                first, second = ref[:, 4 * q + p, :], ref[:, 4 * q + 2 + p, :]
                even = jnp.where(low_half, first, pltpu.roll(second, 64, 1))
                odd = jnp.where(low_half, pltpu.roll(first, 64, 1), second)
                for a in range(4):
                    out_ref[q, pl.ds(64 * p + row + 2 * a, 1), :] = even[a : a + 1]
                    out_ref[q, pl.ds(64 * p + row + 2 * a + 1, 1), :] = odd[a : a + 1]


def prepare_kernel(s_ref, out_ref):
    half = s_ref.shape[0] // 2
    for step in range(2):
        even, odd = (s_ref[pl.ds(half * step + p, half // 2, stride=2), :] for p in range(2))
        high, low = split(jnp.transpose(jnp.concatenate([even, odd], axis=1)))
        out_ref[step, :128] = high
        out_ref[step, 128:] = low


def sketch_kernel(r_ref, d_ref, s_ref, gram_ref, z_ref, acc_ref):
    step = pl.program_id(0)
    depth = r_ref.shape[0] // 8
    s_both = s_ref[0]
    s_high = s_both[:128]

    @pl.when(step == 0)
    def _():
        acc_ref[...] = jnp.zeros_like(acc_ref)

    for pair in range(4):
        block = jnp.concatenate([r_ref[pl.ds(2 * pair + p, depth, stride=8), :] for p in range(2)], axis=1)
        high, low = split(block)
        both = mm(s_both, high, NN)
        acc_ref[pair] += both[:128] + both[128:] + mm(s_high, low, NN)

    @pl.when(step == pl.num_programs(0) - 1)
    def _():
        low_half = low_lanes((64, 128))
        squares = []
        diagonals = []
        row = lax.broadcasted_iota(jnp.int32, (64, 128), 0)
        lane = lax.broadcasted_iota(jnp.int32, (64, 128), 1)
        for q in range(2):
            halves = []
            for f in range(2):
                sums = acc_ref[2 * q + f]
                x, y = sums[:, :128], sums[:, 128:]
                halves.append(
                    jnp.where(
                        low_half,
                        x[:64] + pltpu.roll(x[64:], 64, 1),
                        pltpu.roll(y[:64], 64, 1) + y[64:],
                    )
                )
            reverse = jnp.transpose(jnp.concatenate(halves, axis=0))
            z = 0.5 * (d_ref[q] + reverse)
            z_ref[q] = z
            gram = lax.dot_general(
                z, z, (((0,), (0,)), ((), ())), precision=lax.Precision.HIGHEST, preferred_element_type=F32
            )
            lower, upper = gram[:64], gram[64:]
            if q == 0:
                upper = pltpu.roll(upper, 64, 1)
            else:
                lower = pltpu.roll(lower, 64, 1)
            squares.append(jnp.where(lane - 64 * q <= row, lower, upper))
            diagonals.append(jnp.sum(jnp.where(lane - 64 * q == row, upper, 0.0), axis=0, keepdims=True))
        gram_ref[:64] = jnp.where(low_half, squares[0], squares[1])
        gram_ref[64:] = jnp.where(low_lanes((8, 128)), *(jnp.broadcast_to(d, (8, 128)) for d in diagonals))


def factor_kernel(scaling, g_ref, h_ref, z_ref, basis_ref, r_ref, u_ref, l_ref):
    lane = lax.broadcasted_iota(jnp.int32, (8, 128), 1)
    sub = lax.broadcasted_iota(jnp.int32, (8, 128), 0)
    base = lane - lane % 64
    inner = lane % 64
    low_half = low_lanes((64, 128))
    packed = g_ref[...] + h_ref[...]
    square, diagonal = packed[:64], packed[64:65]
    turned = pltpu.roll(square, 64, 1)
    squares = jnp.where(low_half, square, turned), jnp.where(low_half, turned, square)
    flipped = jnp.transpose(jnp.concatenate(squares, axis=0))[:64]
    turned = pltpu.roll(flipped, 64, 1)
    flips = jnp.where(low_half, flipped, turned), jnp.where(low_half, turned, flipped)
    diagonals = pltpu.roll(packed[64:], 64, 1)[:1], diagonal
    row = lax.broadcasted_iota(jnp.int32, (64, 128), 0)
    column = lax.broadcasted_iota(jnp.int32, (64, 128), 1) % 64
    kept = jnp.logical_xor(column > row, low_half)
    g = []
    for q in range(2):
        full = jnp.where(kept, squares[q], flips[q])
        full = jnp.where(jnp.logical_and(column == row, jnp.logical_not(low_half)), diagonals[q], full)
        g.append([full[8 * b : 8 * b + 8] for b in range(8)])
    e = [[jnp.where(inner == sub + 8 * b, 1.0, 0.0).astype(F32) for b in range(8)] for _ in range(2)]

    def spread(x, row):
        return jnp.broadcast_to(x[row : row + 1], (8, 128))

    for top in range(8):
        cols = [
            [[jnp.take_along_axis(g[q][b], base + (8 * top + a), axis=1) for b in range(top, 8)] for a in range(8)]
            for q in range(2)
        ]
        for a in range(8):
            j = 8 * top + a
            for q in range(2):
                pivot = spread(cols[q][a][0], a)
                inverse = 1.0 / pivot
                mult = [x * inverse for x in cols[q][a]]
                for later in range(a + 1, 8):
                    weight = spread(cols[q][later][0], a)
                    cols[q][later] = [x - m * weight for x, m in zip(cols[q][later], mult)]
                grow = spread(g[q][top], a)
                erow = spread(e[q][top], a)
                scale = lax.rsqrt(pivot)
                scale = scale * (1.5 - 0.5 * pivot * scale * scale)
                u_ref[q, j : j + 1, :] = jnp.where(inner >= j, grow * scale, 0.0)[:1]
                l_ref[q, j : j + 1, :] = (erow * scale)[:1]
                mult[0] = jnp.where(sub > a, mult[0], 0.0)
                for b in range(top, 8):
                    g[q][b] = g[q][b] - mult[b - top] * grow
                    e[q][b] = e[q][b] - mult[b - top] * erow
    for q in range(2):
        u = u_ref[q] * (1.0 / scaling)
        r_ref[2 * q] = u[:, :64]
        r_ref[2 * q + 1] = pltpu.roll(u, 64, 1)[:, :64]
        inv = l_ref[q]
        inv = jnp.concatenate([jnp.where(low_half, inv, 0.0), jnp.where(low_half, 0.0, inv)], axis=0)
        out = lax.dot_general(z_ref[q], inv, NT, precision=lax.Precision.HIGHEST, preferred_element_type=F32) * scaling
        turned = pltpu.roll(out, 64, 1)
        for p in range(2):
            basis_ref[2 * q, p] = out[64 * p : 64 * p + 64, :64]
            basis_ref[2 * q + 1, p] = turned[64 * p : 64 * p + 64, :64]


def local(traces, sketch):
    shots, receivers, samples = traces.shape
    devices = lax.axis_size("src") * lax.axis_size("rcv")
    rcv_count = lax.axis_size("rcv")
    weights = dft_rows(samples)
    w_high = weights.astype(BF16)
    w_low = (weights - w_high.astype(np.float32)).astype(BF16)
    w_both = jnp.asarray(np.concatenate([w_high, w_low], axis=0))
    sd = jax.ShapeDtypeStruct
    spec = pl.pallas_call(
        dft_kernel,
        in_specs=[pl.BlockSpec(memory_space=pltpu.HBM)] * 2,
        out_specs=pl.BlockSpec(memory_space=pltpu.HBM),
        out_shape=sd((devices, 4, 8, 128), F32),
        scratch_shapes=[
            pltpu.VMEM((shots, receivers, samples), F32),
            pltpu.VMEM((128, samples), BF16),
            pltpu.VMEM((devices, 4, 8, 128), F32),
            pltpu.SemaphoreType.DMA((receivers // 128,)),
            pltpu.SemaphoreType.DMA,
            pltpu.SemaphoreType.DMA((receivers // 128,)),
        ],
        cost_estimate=pl.CostEstimate(flops=3 * 2 * 64 * 8192 * 512, bytes_accessed=19 << 20, transcendentals=0),
        name="dft",
    )(traces, w_both)
    received = lax.all_to_all(spec.reshape(devices, 32, 128), ("src", "rcv"), split_axis=0, concat_axis=0, tiled=True)
    own = pl.pallas_call(
        own_kernel,
        grid=(2,),
        in_specs=[
            pl.BlockSpec((devices // 2, 4, 8, 128), lambda g: (g, 0, 0, 0)),
            pl.BlockSpec((RANK, receivers // 2), lambda g: (0, g)),
        ],
        out_specs=[pl.BlockSpec((4, 8, 128), lambda g: (0, 0, 0))] * rcv_count,
        out_shape=[sd((4, 8, 128), F32)] * rcv_count,
        scratch_shapes=[pltpu.VMEM((rcv_count, 4, 8, 128), F32)],
        cost_estimate=pl.CostEstimate(flops=3 << 30, bytes_accessed=4 << 20, transcendentals=0),
        name="own",
        **small(8),
    )
    prepared = pl.pallas_call(
        prepare_kernel, out_shape=sd((2, 256, receivers // 4), BF16), name="prepare", **small(8)
    )(sketch)
    pieces = list(own(pltpu.with_memory_space_constraint(spec, pltpu.HBM), sketch.T))
    for slot in range(1, rcv_count):
        pairs = [(r, r ^ slot) for r in range(rcv_count)]
        pieces[slot] = lax.ppermute(pieces[slot], "rcv", pairs)
    direct = pl.pallas_call(place_kernel, out_shape=sd((2, 128, 128), F32), name="place", **small(8))(*pieces)
    gram, z = pl.pallas_call(
        sketch_kernel,
        grid=(2,),
        in_specs=[
            pl.BlockSpec((devices * 16, 128), lambda g: (g, 0)),
            pl.BlockSpec((2, 128, 128), lambda g: (0, 0, 0)),
            pl.BlockSpec((1, 256, receivers // 4), lambda g: (g, 0, 0)),
        ],
        out_specs=[pl.BlockSpec((72, 128), lambda g: (0, 0)), pl.BlockSpec((2, 128, 128), lambda g: (0, 0, 0))],
        out_shape=[sd((72, 128), F32), sd((2, 128, 128), F32)],
        scratch_shapes=[pltpu.VMEM((4, 128, 256), F32)],
        name="sketch",
        **small(12),
    )(pltpu.with_memory_space_constraint(received.reshape(devices * 32, 128), pltpu.VMEM), direct, prepared)
    src = lax.axis_size("src")
    for bits in (1, 9, 3):
        gram = gram + lax.ppermute(gram, "src", [(s, s ^ bits) for s in range(src)])
    other = lax.ppermute(gram, "src", [(s, s ^ 7) for s in range(src)])
    scaling = math.sqrt(2.0 * receivers)
    basis, r_factor = pl.pallas_call(
        lambda *refs: factor_kernel(scaling, *refs),
        out_shape=[sd((4, 2, 64, 64), F32), sd((4, 64, 64), F32)],
        scratch_shapes=[pltpu.VMEM((2, 64, 128), F32), pltpu.VMEM((2, 64, 128), F32)],
        name="factor",
        **small(8),
    )(gram, other, z)
    return basis, r_factor


def solution(mesh):
    in_specs = (P(("src", "rcv"), None, None), P())
    out_specs = (P("rcv", None, "src", None), P("rcv", None, None))
    return jax.shard_map(local, mesh=mesh, in_specs=in_specs, out_specs=out_specs, check_vma=False)
```

```python
import math

import jax
import jax.numpy as jnp
import numpy as np
from jax import lax
from jax.experimental import pallas as pl
from jax.experimental.pallas import tpu as pltpu
from jax.sharding import PartitionSpec as P


FREQS = 32
RANK = 64
F32 = jnp.float32
BF16 = jnp.bfloat16
NT = (((1,), (1,)), ((), ()))
NN = (((1,), (0,)), ((), ()))


def dft_rows(samples):
    times = np.arange(samples)
    orders = np.arange(1, FREQS + 1)
    angles = (orders[:, None] * times[None, :] % samples) * (2.0 * math.pi / samples)
    weights = np.stack([np.cos(angles), -np.sin(angles)], axis=1)
    return (weights.reshape(2 * FREQS, samples) / math.sqrt(samples)).astype(np.float32)


def small(mib):
    return dict(compiler_params=pltpu.CompilerParams(vmem_limit_bytes=mib << 20))


def split(x):
    high = x.astype(BF16)
    return high, (x - high.astype(F32)).astype(BF16)


def mm(a, b, dims):
    return lax.dot_general(a, b, dims, preferred_element_type=F32)


def low_lanes(shape):
    return lax.broadcasted_iota(jnp.int32, shape, 1) < 64


SPANS = (2, 4, 4, 4, 2)


def dft_kernel(x_hbm, w_hbm, spec_hbm, x_ref, w_ref, out_ref, x_sems, w_sem, out_sems):
    starts = [sum(SPANS[:k]) for k in range(len(SPANS))]
    ahead = 2

    def fetch(step):
        span = pl.ds(64 * starts[step], 64 * SPANS[step])
        return pltpu.make_async_copy(x_hbm.at[:, span, :], x_ref.at[:, span, :], x_sems.at[step])

    def put(step):
        span = pl.ds(8 * starts[step], 8 * SPANS[step])
        return pltpu.make_async_copy(out_ref.at[span], spec_hbm.at[span], out_sems.at[step])

    w_copy = pltpu.make_async_copy(w_hbm, w_ref, w_sem)
    w_copy.start()
    for step in range(ahead):
        fetch(step).start()
    w_copy.wait()
    for step in range(len(SPANS)):
        fetch(step).wait()
        if step + ahead < len(SPANS):
            fetch(step + ahead).start()
        weights = w_ref[...]
        for tile in range(starts[step], starts[step] + SPANS[step]):
            for half in range(2):
                x = x_ref[4 * half : 4 * half + 4, 64 * tile : 64 * tile + 64, :]
                high, low = split(x.reshape(256, -1))
                both = mm(weights, high, NT)
                out = both[:64] + both[64:] + mm(weights[:64], low, NT)
                for c in range(2):
                    piece = out[:, 128 * c : 128 * c + 128]
                    out_ref[8 * tile : 8 * tile + 8, 2 * half + c] = piece.reshape(8, 8, 128)
        put(step).start()
    for step in range(len(SPANS)):
        put(step).wait()


def own_kernel(spec_ref, st_ref, *refs):
    d_ref = refs[-1]
    low_half = low_lanes((64, 128))
    zero = jnp.zeros((64, 128), F32)
    total = None
    for g in range(spec_ref.shape[0] // 16):
        rows = jnp.concatenate(
            [
                jnp.concatenate(
                    [spec_ref[16 * g + 8 * t : 16 * g + 8 * t + 8, a].reshape(64, 128) for t in range(2)], axis=1
                )
                for a in range(4)
            ],
            axis=0,
        )
        st = st_ref[:, 128 * g : 128 * g + 128]
        rolled = pltpu.roll(st, 64, 1)
        even = jnp.concatenate([jnp.where(low_half, st, zero), jnp.where(low_half, rolled, zero)], axis=1)
        odd = jnp.concatenate([jnp.where(low_half, zero, rolled), jnp.where(low_half, zero, st)], axis=1)
        s_high, s_low = split(jnp.concatenate([even, odd], axis=0))
        high, low = split(rows)
        both = mm(high, jnp.concatenate([s_high, s_low], axis=0), NT)
        out = both[:, :128] + both[:, 128:] + mm(low, s_high, NT)
        total = out if total is None else total + out

    @pl.when(pl.program_id(0) == 0)
    def _():
        d_ref[...] = jnp.zeros_like(d_ref)

    for a in range(4):
        d_ref[:, a] += total[64 * a : 64 * a + 64].reshape(8, 8, 128)

    @pl.when(pl.program_id(0) == pl.num_programs(0) - 1)
    def _():
        me = lax.axis_index("rcv")
        for slot, ref in enumerate(refs[:-1]):
            ref[...] = d_ref[slot ^ me]


def place_kernel(*refs):
    out_ref = refs[-1]
    me = lax.axis_index("rcv")
    low_half = low_lanes((4, 128))
    for slot, ref in enumerate(refs[:-1]):
        row = pl.multiple_of(8 * (slot ^ me), 8)
        for q in range(2):
            for p in range(2):
                first, second = ref[:, 4 * q + p, :], ref[:, 4 * q + 2 + p, :]
                even = jnp.where(low_half, first, pltpu.roll(second, 64, 1))
                odd = jnp.where(low_half, pltpu.roll(first, 64, 1), second)
                for a in range(4):
                    out_ref[q, pl.ds(64 * p + row + 2 * a, 1), :] = even[a : a + 1]
                    out_ref[q, pl.ds(64 * p + row + 2 * a + 1, 1), :] = odd[a : a + 1]


def prepare_kernel(s_ref, out_ref):
    even, odd = (s_ref[pl.ds(p, s_ref.shape[0] // 2, stride=2), :] for p in range(2))
    high, low = split(jnp.transpose(jnp.concatenate([even, odd], axis=1)))
    out_ref[:128] = high
    out_ref[128:] = low


def sketch_kernel(r_ref, d_ref, s_ref, gram_ref, z_ref):
    depth = r_ref.shape[0] // 8
    s_both = s_ref[...]
    s_high = s_both[:128]
    sums = []
    for pair in range(4):
        block = jnp.concatenate([r_ref[pl.ds(2 * pair + p, depth, stride=8), :] for p in range(2)], axis=1)
        high, low = split(block)
        both = mm(s_both, high, NN)
        sums.append(both[:128] + both[128:] + mm(s_high, low, NN))
    low_half = low_lanes((64, 128))
    squares = []
    diagonals = []
    row = lax.broadcasted_iota(jnp.int32, (64, 128), 0)
    lane = lax.broadcasted_iota(jnp.int32, (64, 128), 1)
    for q in range(2):
        halves = []
        for f in range(2):
            x, y = sums[2 * q + f][:, :128], sums[2 * q + f][:, 128:]
            halves.append(
                jnp.where(
                    low_half,
                    x[:64] + pltpu.roll(x[64:], 64, 1),
                    pltpu.roll(y[:64], 64, 1) + y[64:],
                )
            )
        reverse = jnp.transpose(jnp.concatenate(halves, axis=0))
        z = 0.5 * (d_ref[q] + reverse)
        z_ref[q] = z
        gram = lax.dot_general(
            z, z, (((0,), (0,)), ((), ())), precision=lax.Precision.HIGHEST, preferred_element_type=F32
        )
        lower, upper = gram[:64], gram[64:]
        if q == 0:
            upper = pltpu.roll(upper, 64, 1)
        else:
            lower = pltpu.roll(lower, 64, 1)
        squares.append(jnp.where(lane - 64 * q <= row, lower, upper))
        diagonals.append(jnp.sum(jnp.where(lane - 64 * q == row, upper, 0.0), axis=0, keepdims=True))
    gram_ref[:64] = jnp.where(low_half, squares[0], squares[1])
    gram_ref[64:] = jnp.where(low_lanes((8, 128)), *(jnp.broadcast_to(d, (8, 128)) for d in diagonals))


def factor_kernel(scaling, g_ref, h_ref, z_ref, basis_ref, r_ref, u_ref, l_ref):
    lane = lax.broadcasted_iota(jnp.int32, (8, 128), 1)
    sub = lax.broadcasted_iota(jnp.int32, (8, 128), 0)
    base = lane - lane % 64
    inner = lane % 64
    low_half = low_lanes((64, 128))
    packed = g_ref[...] + h_ref[...]
    square, diagonal = packed[:64], packed[64:65]
    turned = pltpu.roll(square, 64, 1)
    squares = jnp.where(low_half, square, turned), jnp.where(low_half, turned, square)
    flipped = jnp.transpose(jnp.concatenate(squares, axis=0))[:64]
    turned = pltpu.roll(flipped, 64, 1)
    flips = jnp.where(low_half, flipped, turned), jnp.where(low_half, turned, flipped)
    diagonals = pltpu.roll(packed[64:], 64, 1)[:1], diagonal
    row = lax.broadcasted_iota(jnp.int32, (64, 128), 0)
    column = lax.broadcasted_iota(jnp.int32, (64, 128), 1) % 64
    kept = jnp.logical_xor(column > row, low_half)
    g = []
    for q in range(2):
        full = jnp.where(kept, squares[q], flips[q])
        full = jnp.where(jnp.logical_and(column == row, jnp.logical_not(low_half)), diagonals[q], full)
        g.append([full[8 * b : 8 * b + 8] for b in range(8)])
    e = [[jnp.where(inner == sub + 8 * b, 1.0, 0.0).astype(F32) for b in range(8)] for _ in range(2)]

    def spread(x, row):
        return jnp.broadcast_to(x[row : row + 1], (8, 128))

    for top in range(8):
        cols = [
            [[jnp.take_along_axis(g[q][b], base + (8 * top + a), axis=1) for b in range(top, 8)] for a in range(8)]
            for q in range(2)
        ]
        for a in range(8):
            j = 8 * top + a
            for q in range(2):
                pivot = spread(cols[q][a][0], a)
                inverse = 1.0 / pivot
                mult = [x * inverse for x in cols[q][a]]
                for later in range(a + 1, 8):
                    weight = spread(cols[q][later][0], a)
                    cols[q][later] = [x - m * weight for x, m in zip(cols[q][later], mult)]
                grow = spread(g[q][top], a)
                erow = spread(e[q][top], a)
                scale = lax.rsqrt(pivot)
                scale = scale * (1.5 - 0.5 * pivot * scale * scale)
                u_ref[q, j : j + 1, :] = jnp.where(inner >= j, grow * scale, 0.0)[:1]
                l_ref[q, j : j + 1, :] = (erow * scale)[:1]
                mult[0] = jnp.where(sub > a, mult[0], 0.0)
                for b in range(top, 8):
                    g[q][b] = g[q][b] - mult[b - top] * grow
                    e[q][b] = e[q][b] - mult[b - top] * erow
    for q in range(2):
        u = u_ref[q] * (1.0 / scaling)
        r_ref[2 * q] = u[:, :64]
        r_ref[2 * q + 1] = pltpu.roll(u, 64, 1)[:, :64]
        inv = l_ref[q]
        inv = jnp.concatenate([jnp.where(low_half, inv, 0.0), jnp.where(low_half, 0.0, inv)], axis=0)
        out = lax.dot_general(z_ref[q], inv, NT, precision=lax.Precision.HIGHEST, preferred_element_type=F32) * scaling
        turned = pltpu.roll(out, 64, 1)
        for p in range(2):
            basis_ref[2 * q, p] = out[64 * p : 64 * p + 64, :64]
            basis_ref[2 * q + 1, p] = turned[64 * p : 64 * p + 64, :64]


def local(traces, sketch):
    shots, receivers, samples = traces.shape
    devices = lax.axis_size("src") * lax.axis_size("rcv")
    rcv_count = lax.axis_size("rcv")
    weights = dft_rows(samples)
    w_high = weights.astype(BF16)
    w_low = (weights - w_high.astype(np.float32)).astype(BF16)
    w_both = jnp.asarray(np.concatenate([w_high, w_low], axis=0))
    sd = jax.ShapeDtypeStruct
    spec = pl.pallas_call(
        dft_kernel,
        in_specs=[pl.BlockSpec(memory_space=pltpu.HBM)] * 2,
        out_specs=pl.BlockSpec(memory_space=pltpu.HBM),
        out_shape=sd((devices, 4, 8, 128), F32),
        scratch_shapes=[
            pltpu.VMEM((shots, receivers, samples), F32),
            pltpu.VMEM((128, samples), BF16),
            pltpu.VMEM((devices, 4, 8, 128), F32),
            pltpu.SemaphoreType.DMA((len(SPANS),)),
            pltpu.SemaphoreType.DMA,
            pltpu.SemaphoreType.DMA((len(SPANS),)),
        ],
        cost_estimate=pl.CostEstimate(flops=3 * 2 * 64 * 8192 * 512, bytes_accessed=19 << 20, transcendentals=0),
        name="dft",
    )(traces, w_both)
    received = lax.all_to_all(spec.reshape(devices, 32, 128), ("src", "rcv"), split_axis=0, concat_axis=0, tiled=True)
    own = pl.pallas_call(
        own_kernel,
        grid=(2,),
        in_specs=[
            pl.BlockSpec((devices // 2, 4, 8, 128), lambda g: (g, 0, 0, 0)),
            pl.BlockSpec((RANK, receivers // 2), lambda g: (0, g)),
        ],
        out_specs=[pl.BlockSpec((4, 8, 128), lambda g: (0, 0, 0))] * rcv_count,
        out_shape=[sd((4, 8, 128), F32)] * rcv_count,
        scratch_shapes=[pltpu.VMEM((rcv_count, 4, 8, 128), F32)],
        cost_estimate=pl.CostEstimate(flops=3 << 30, bytes_accessed=4 << 20, transcendentals=0),
        name="own",
        **small(8),
    )
    prepared = pl.pallas_call(
        prepare_kernel, out_shape=sd((256, receivers // 2), BF16), name="prepare", **small(8)
    )(sketch)
    pieces = list(own(pltpu.with_memory_space_constraint(spec, pltpu.HBM), sketch.T))
    for slot in range(1, rcv_count):
        pairs = [(r, r ^ slot) for r in range(rcv_count)]
        pieces[slot] = lax.ppermute(pieces[slot], "rcv", pairs)
    direct = pl.pallas_call(place_kernel, out_shape=sd((2, 128, 128), F32), name="place", **small(8))(*pieces)
    gram, z = pl.pallas_call(
        sketch_kernel,
        in_specs=[pl.BlockSpec(memory_space=pltpu.VMEM)] * 3,
        out_shape=[sd((72, 128), F32), sd((2, 128, 128), F32)],
        name="sketch",
        **small(12),
    )(pltpu.with_memory_space_constraint(received.reshape(devices * 32, 128), pltpu.VMEM), direct, prepared)
    src = lax.axis_size("src")
    for bits in (1, 9, 3):
        gram = gram + lax.ppermute(gram, "src", [(s, s ^ bits) for s in range(src)])
    other = lax.ppermute(gram, "src", [(s, s ^ 7) for s in range(src)])
    scaling = math.sqrt(2.0 * receivers)
    basis, r_factor = pl.pallas_call(
        lambda *refs: factor_kernel(scaling, *refs),
        out_shape=[sd((4, 2, 64, 64), F32), sd((4, 64, 64), F32)],
        scratch_shapes=[pltpu.VMEM((2, 64, 128), F32), pltpu.VMEM((2, 64, 128), F32)],
        name="factor",
        **small(8),
    )(gram, other, z)
    return basis, r_factor


def solution(mesh):
    in_specs = (P(("src", "rcv"), None, None), P())
    out_specs = (P("rcv", None, "src", None), P("rcv", None, None))
    return jax.shard_map(local, mesh=mesh, in_specs=in_specs, out_specs=out_specs, check_vma=False)
```

```python
import math

import jax
import jax.numpy as jnp
import numpy as np
from jax import lax
from jax.experimental import pallas as pl
from jax.experimental.pallas import tpu as pltpu
from jax.sharding import PartitionSpec as P


FREQS = 32
RANK = 64
F32 = jnp.float32
BF16 = jnp.bfloat16
NT = (((1,), (1,)), ((), ()))
NN = (((1,), (0,)), ((), ()))


def dft_rows(samples):
    times = np.arange(samples)
    orders = np.arange(1, FREQS + 1)
    angles = (orders[:, None] * times[None, :] % samples) * (2.0 * math.pi / samples)
    weights = np.stack([np.cos(angles), -np.sin(angles)], axis=1)
    return (weights.reshape(2 * FREQS, samples) / math.sqrt(samples)).astype(np.float32)


def small(mib):
    return dict(compiler_params=pltpu.CompilerParams(vmem_limit_bytes=mib << 20))


def split(x):
    high = x.astype(BF16)
    return high, (x - high.astype(F32)).astype(BF16)


def mm(a, b, dims):
    return lax.dot_general(a, b, dims, preferred_element_type=F32)


def low_lanes(shape):
    return lax.broadcasted_iota(jnp.int32, shape, 1) < 64


SPANS = (2, 4, 4, 4, 2)


def dft_kernel(x_hbm, w_hbm, spec_hbm, x_ref, w_ref, out_ref, x_sems, w_sem, out_sems):
    starts = [sum(SPANS[:k]) for k in range(len(SPANS))]
    ahead = 2

    def fetch(step):
        span = pl.ds(64 * starts[step], 64 * SPANS[step])
        return pltpu.make_async_copy(x_hbm.at[:, span, :], x_ref.at[:, span, :], x_sems.at[step])

    def put(step):
        span = pl.ds(8 * starts[step], 8 * SPANS[step])
        return pltpu.make_async_copy(out_ref.at[span], spec_hbm.at[span], out_sems.at[step])

    w_copy = pltpu.make_async_copy(w_hbm, w_ref, w_sem)
    w_copy.start()
    for step in range(ahead):
        fetch(step).start()
    w_copy.wait()
    for step in range(len(SPANS)):
        fetch(step).wait()
        if step + ahead < len(SPANS):
            fetch(step + ahead).start()
        weights = w_ref[...]
        for tile in range(starts[step], starts[step] + SPANS[step]):
            for half in range(2):
                x = x_ref[4 * half : 4 * half + 4, 64 * tile : 64 * tile + 64, :]
                high, low = split(x.reshape(256, -1))
                both = mm(weights, high, NT)
                out = both[:64] + both[64:] + mm(weights[:64], low, NT)
                for c in range(2):
                    piece = out[:, 128 * c : 128 * c + 128]
                    out_ref[8 * tile : 8 * tile + 8, 2 * half + c] = piece.reshape(8, 8, 128)
        put(step).start()
    for step in range(len(SPANS)):
        put(step).wait()


def own_kernel(spec_ref, st_ref, *refs):
    d_ref = refs[-1]
    low_half = low_lanes((64, 128))
    zero = jnp.zeros((64, 128), F32)
    total = None
    for g in range(spec_ref.shape[0] // 16):
        rows = jnp.concatenate(
            [
                jnp.concatenate(
                    [spec_ref[16 * g + 8 * t : 16 * g + 8 * t + 8, a].reshape(64, 128) for t in range(2)], axis=1
                )
                for a in range(4)
            ],
            axis=0,
        )
        st = st_ref[:, 128 * g : 128 * g + 128]
        rolled = pltpu.roll(st, 64, 1)
        even = jnp.concatenate([jnp.where(low_half, st, zero), jnp.where(low_half, rolled, zero)], axis=1)
        odd = jnp.concatenate([jnp.where(low_half, zero, rolled), jnp.where(low_half, zero, st)], axis=1)
        s_high, s_low = split(jnp.concatenate([even, odd], axis=0))
        high, low = split(rows)
        both = mm(high, jnp.concatenate([s_high, s_low], axis=0), NT)
        out = both[:, :128] + both[:, 128:] + mm(low, s_high, NT)
        total = out if total is None else total + out

    @pl.when(pl.program_id(0) == 0)
    def _():
        d_ref[...] = jnp.zeros_like(d_ref)

    for a in range(4):
        d_ref[:, a] += total[64 * a : 64 * a + 64].reshape(8, 8, 128)

    @pl.when(pl.program_id(0) == pl.num_programs(0) - 1)
    def _():
        me = lax.axis_index("rcv")
        for slot, ref in enumerate(refs[:-1]):
            ref[...] = d_ref[slot ^ me]


def place_kernel(*refs):
    out_ref = refs[-1]
    me = lax.axis_index("rcv")
    low_half = low_lanes((4, 128))
    for slot, ref in enumerate(refs[:-1]):
        row = pl.multiple_of(8 * (slot ^ me), 8)
        for q in range(2):
            for p in range(2):
                first, second = ref[:, 4 * q + p, :], ref[:, 4 * q + 2 + p, :]
                even = jnp.where(low_half, first, pltpu.roll(second, 64, 1))
                odd = jnp.where(low_half, pltpu.roll(first, 64, 1), second)
                for a in range(4):
                    out_ref[q, pl.ds(64 * p + row + 2 * a, 1), :] = even[a : a + 1]
                    out_ref[q, pl.ds(64 * p + row + 2 * a + 1, 1), :] = odd[a : a + 1]


def prepare_kernel(s_ref, out_ref):
    even, odd = (s_ref[pl.ds(p, s_ref.shape[0] // 2, stride=2), :] for p in range(2))
    high, low = split(jnp.transpose(jnp.concatenate([even, odd], axis=1)))
    out_ref[:128] = high
    out_ref[128:] = low


def sketch_kernel(r_ref, d_ref, s_ref, gram_ref, z_ref):
    depth = r_ref.shape[0] // 8
    s_both = s_ref[...]
    s_high = s_both[:128]
    sums = []
    for pair in range(4):
        block = jnp.concatenate([r_ref[pl.ds(2 * pair + p, depth, stride=8), :] for p in range(2)], axis=1)
        high, low = split(block)
        both = mm(s_both, high, NN)
        sums.append(both[:128] + both[128:] + mm(s_high, low, NN))
    low_half = low_lanes((64, 128))
    squares = []
    diagonals = []
    row = lax.broadcasted_iota(jnp.int32, (64, 128), 0)
    lane = lax.broadcasted_iota(jnp.int32, (64, 128), 1)
    for q in range(2):
        halves = []
        for f in range(2):
            x, y = sums[2 * q + f][:, :128], sums[2 * q + f][:, 128:]
            halves.append(
                jnp.where(
                    low_half,
                    x[:64] + pltpu.roll(x[64:], 64, 1),
                    pltpu.roll(y[:64], 64, 1) + y[64:],
                )
            )
        reverse = jnp.transpose(jnp.concatenate(halves, axis=0))
        z = 0.5 * (d_ref[q] + reverse)
        z_ref[q] = z
        gram = lax.dot_general(
            z, z, (((0,), (0,)), ((), ())), precision=lax.Precision.HIGHEST, preferred_element_type=F32
        )
        lower, upper = gram[:64], gram[64:]
        if q == 0:
            upper = pltpu.roll(upper, 64, 1)
        else:
            lower = pltpu.roll(lower, 64, 1)
        squares.append(jnp.where(lane - 64 * q <= row, lower, upper))
        diagonals.append(jnp.sum(jnp.where(lane - 64 * q == row, upper, 0.0), axis=0, keepdims=True))
    gram_ref[:64] = jnp.where(low_half, squares[0], squares[1])
    gram_ref[64:] = jnp.where(low_lanes((8, 128)), *(jnp.broadcast_to(d, (8, 128)) for d in diagonals))


def factor_kernel(scaling, g_ref, h_ref, z_ref, basis_ref, r_ref, u_ref, l_ref):
    lane = lax.broadcasted_iota(jnp.int32, (8, 128), 1)
    sub = lax.broadcasted_iota(jnp.int32, (8, 128), 0)
    base = lane - lane % 64
    inner = lane % 64
    low_half = low_lanes((64, 128))
    packed = g_ref[...] + h_ref[...]
    square, diagonal = packed[:64], packed[64:65]
    turned = pltpu.roll(square, 64, 1)
    squares = jnp.where(low_half, square, turned), jnp.where(low_half, turned, square)
    flipped = jnp.transpose(jnp.concatenate(squares, axis=0))[:64]
    turned = pltpu.roll(flipped, 64, 1)
    flips = jnp.where(low_half, flipped, turned), jnp.where(low_half, turned, flipped)
    diagonals = pltpu.roll(packed[64:], 64, 1)[:1], diagonal
    row = lax.broadcasted_iota(jnp.int32, (64, 128), 0)
    column = lax.broadcasted_iota(jnp.int32, (64, 128), 1) % 64
    kept = jnp.logical_xor(column > row, low_half)
    g = []
    for q in range(2):
        full = jnp.where(kept, squares[q], flips[q])
        full = jnp.where(jnp.logical_and(column == row, jnp.logical_not(low_half)), diagonals[q], full)
        g.append([full[8 * b : 8 * b + 8] for b in range(8)])
    e = [[jnp.where(inner == sub + 8 * b, 1.0, 0.0).astype(F32) for b in range(8)] for _ in range(2)]

    def spread(x, row):
        return jnp.broadcast_to(x[row : row + 1], (8, 128))

    for top in range(8):
        cols = [
            [[jnp.take_along_axis(g[q][b], base + (8 * top + a), axis=1) for b in range(top, 8)] for a in range(8)]
            for q in range(2)
        ]
        for a in range(8):
            j = 8 * top + a
            for q in range(2):
                pivot = spread(cols[q][a][0], a)
                inverse = 1.0 / pivot
                mult = [x * inverse for x in cols[q][a]]
                for later in range(a + 1, 8):
                    weight = spread(cols[q][later][0], a)
                    cols[q][later] = [x - m * weight for x, m in zip(cols[q][later], mult)]
                grow = spread(g[q][top], a)
                erow = spread(e[q][top], a)
                scale = lax.rsqrt(pivot)
                scale = scale * (1.5 - 0.5 * pivot * scale * scale)
                u_ref[q, j : j + 1, :] = jnp.where(inner >= j, grow * scale, 0.0)[:1]
                l_ref[q, j : j + 1, :] = (erow * scale)[:1]
                mult[0] = jnp.where(sub > a, mult[0], 0.0)
                for b in range(top, 8):
                    g[q][b] = g[q][b] - mult[b - top] * grow
                    e[q][b] = e[q][b] - mult[b - top] * erow
    for q in range(2):
        u = u_ref[q] * (1.0 / scaling)
        r_ref[2 * q] = u[:, :64]
        r_ref[2 * q + 1] = pltpu.roll(u, 64, 1)[:, :64]
        inv = l_ref[q]
        inv = jnp.concatenate([jnp.where(low_half, inv, 0.0), jnp.where(low_half, 0.0, inv)], axis=0)
        out = lax.dot_general(z_ref[q], inv, NT, precision=lax.Precision.HIGHEST, preferred_element_type=F32) * scaling
        turned = pltpu.roll(out, 64, 1)
        for p in range(2):
            basis_ref[2 * q, p] = out[64 * p : 64 * p + 64, :64]
            basis_ref[2 * q + 1, p] = turned[64 * p : 64 * p + 64, :64]


def local(traces, sketch):
    shots, receivers, samples = traces.shape
    devices = lax.axis_size("src") * lax.axis_size("rcv")
    rcv_count = lax.axis_size("rcv")
    weights = dft_rows(samples)
    w_high = weights.astype(BF16)
    w_low = (weights - w_high.astype(np.float32)).astype(BF16)
    w_both = jnp.asarray(np.concatenate([w_high, w_low], axis=0))
    sd = jax.ShapeDtypeStruct
    spec = pl.pallas_call(
        dft_kernel,
        in_specs=[pl.BlockSpec(memory_space=pltpu.HBM)] * 2,
        out_specs=pl.BlockSpec(memory_space=pltpu.HBM),
        out_shape=sd((devices, 4, 8, 128), F32),
        scratch_shapes=[
            pltpu.VMEM((shots, receivers, samples), F32),
            pltpu.VMEM((128, samples), BF16),
            pltpu.VMEM((devices, 4, 8, 128), F32),
            pltpu.SemaphoreType.DMA((len(SPANS),)),
            pltpu.SemaphoreType.DMA,
            pltpu.SemaphoreType.DMA((len(SPANS),)),
        ],
        cost_estimate=pl.CostEstimate(flops=3 * 2 * 64 * 8192 * 512, bytes_accessed=19 << 20, transcendentals=0),
        name="dft",
    )(traces, w_both)
    received = lax.all_to_all(spec.reshape(devices, 32, 128), ("src", "rcv"), split_axis=0, concat_axis=0, tiled=True)
    own = pl.pallas_call(
        own_kernel,
        grid=(4,),
        in_specs=[
            pl.BlockSpec((devices // 4, 4, 8, 128), lambda g: (g, 0, 0, 0)),
            pl.BlockSpec((RANK, receivers // 4), lambda g: (0, g)),
        ],
        out_specs=[pl.BlockSpec((4, 8, 128), lambda g: (0, 0, 0))] * rcv_count,
        out_shape=[sd((4, 8, 128), F32)] * rcv_count,
        scratch_shapes=[pltpu.VMEM((rcv_count, 4, 8, 128), F32)],
        cost_estimate=pl.CostEstimate(flops=3 << 30, bytes_accessed=4 << 20, transcendentals=0),
        name="own",
        **small(8),
    )
    prepared = pl.pallas_call(
        prepare_kernel, out_shape=sd((256, receivers // 2), BF16), name="prepare", **small(8)
    )(sketch)
    pieces = list(own(pltpu.with_memory_space_constraint(spec, pltpu.HBM), sketch.T))
    for slot in range(1, rcv_count):
        pairs = [(r, r ^ slot) for r in range(rcv_count)]
        pieces[slot] = lax.ppermute(pieces[slot], "rcv", pairs)
    direct = pl.pallas_call(place_kernel, out_shape=sd((2, 128, 128), F32), name="place", **small(8))(*pieces)
    gram, z = pl.pallas_call(
        sketch_kernel,
        in_specs=[pl.BlockSpec(memory_space=pltpu.VMEM)] * 3,
        out_shape=[sd((72, 128), F32), sd((2, 128, 128), F32)],
        name="sketch",
        **small(12),
    )(pltpu.with_memory_space_constraint(received.reshape(devices * 32, 128), pltpu.VMEM), direct, prepared)
    src = lax.axis_size("src")
    for bits in (1, 9, 3):
        gram = gram + lax.ppermute(gram, "src", [(s, s ^ bits) for s in range(src)])
    other = lax.ppermute(gram, "src", [(s, s ^ 7) for s in range(src)])
    scaling = math.sqrt(2.0 * receivers)
    basis, r_factor = pl.pallas_call(
        lambda *refs: factor_kernel(scaling, *refs),
        out_shape=[sd((4, 2, 64, 64), F32), sd((4, 64, 64), F32)],
        scratch_shapes=[pltpu.VMEM((2, 64, 128), F32), pltpu.VMEM((2, 64, 128), F32)],
        name="factor",
        **small(8),
    )(gram, other, z)
    return basis, r_factor


def solution(mesh):
    in_specs = (P(("src", "rcv"), None, None), P())
    out_specs = (P("rcv", None, "src", None), P("rcv", None, None))
    return jax.shard_map(local, mesh=mesh, in_specs=in_specs, out_specs=out_specs, check_vma=False)
```
